256 devices in a mesh: exp: 64 (over z, x, core), seq: 4 (over y).
Axes of the slice: x: 4, y: 4, z: 8, core: 2. Of those that a mesh axis runs over, the one named last changes fastest.
Arguments:
- layer_output_gradient: bfloat16 [2048, 7168], P(('exp', 'seq')), may hold values from -24 to 24
- residual_input: bfloat16 [2048, 7168], P(('exp', 'seq')), may hold values from -6 to 6
- norm_scale_vector: bfloat16 [7168], replicated, may hold values from 0.5 to 1.5
- chosen_expert_index: int32 [2048, 8], P(('exp', 'seq')), may hold values from 0 to 63, all different within a row; in each aligned block of 32 rows (0 to 31, 32 to 63, ...) at most 8 rows name the same one
- routing_gate_weight: bfloat16 [2048, 8], P(('exp', 'seq')), may hold values from 0.099609375 to 0.59765625
- expert_gate_weight: bfloat16 [64, 7168, 1024], P('exp', None, 'seq'), may hold values from -0.0625 to 0.0625
- expert_up_weight: bfloat16 [64, 7168, 1024], P('exp', None, 'seq'), may hold values from -0.0625 to 0.0625
- expert_down_weight: bfloat16 [64, 1024, 7168], P('exp', 'seq'), may hold values from -0.1875 to 0.1875
- stored_gate_state: bfloat16 [64, 512, 1024], P('exp', None, 'seq'), may hold values from -6 to 6
- stored_up_state: bfloat16 [64, 512, 1024], P('exp', None, 'seq'), may hold values from -6 to 6
- attention_output: bfloat16 [2048, 16384], P(('exp', 'seq')), may hold values from -24 to 24
- saved_adapter_latent: bfloat16 [2048, 32], P(('exp', 'seq')), may hold values from -0.109375 to 0.109375
- adapter_up_matrix: bfloat16 [32, 7168], replicated, may hold values from -0.00048828125 to 0.00048828125
Outputs:
- hidden_state_gradient: bfloat16 [2048, 7168], P(('exp', 'seq'))
- adapter_down_gradient: float32 [16384, 32], P(('exp', 'seq'))
- adapter_up_gradient_transposed: float32 [7168, 32], P(('exp', 'seq'))
The draws below stay inside these ranges and needn't reach their ends.
Inputs may be any that keep to these rules, and one draw needn't show every extreme that they name: `chosen_expert_index`: each row names 8 different experts. In each aligned block of 32 rows (the tokens of one index of exp) no expert is named by more than 8 rows, and in some block some expert is named by exactly 8 rows.
All inputs are finite; a program needn't handle non-finite values.
Results may differ from the reference program's by a relative error of at most 0.015.
Values may be sent and summed in bfloat16 or wider, within the bound.
A program may use at most 128 MiB of HBM per device.

```python
import math
import jax
import jax.numpy as jnp
import numpy as np
from jax import lax

MODEL_DIM = 7168
FF = 1024
HEADS = 128
VDIM = 128
ADAPTER_RANK = 32
TOP = 8
GROUP = 32
TOTAL_TOKENS = 2048
EXPERTS = 64
CAP = 8
SLOTS = 512
FF_DEV = 256
N_SEQ = 4


def strengthened(values, rng, source, target, parts, factor):
    owner, partner = [(jnp.arange(values.shape[dim]) // (values.shape[dim] // parts)).reshape([-1 if axis == dim else 1 for axis in range(values.ndim)]) for dim in (source, target)]
    chosen = jax.random.permutation(rng, parts)[partner]
    strong = (owner == chosen) | (owner == (partner + parts // 2) % parts)
    return jnp.where(strong, factor * values, values)


def block_scale(own_key, shape, shards, smallest, largest):
    def one(dim, shards_of):
        steps = jax.random.uniform(jax.random.fold_in(jax.random.fold_in(own_key, 6), dim), (shards_of,), jnp.float32, smallest / len(shards), largest / len(shards))
        return jnp.repeat(jnp.exp(steps), shape[dim] // shards_of).reshape((-1,) + (1,) * (len(shape) - dim - 1))

    level = one(*shards[0])
    for cut in shards[1:]:
        level = level * one(*cut)
    return level


def routed_block(own_key, own, number, rows, number_of, top, limit, lean):
    sequence = jax.random.permutation(own_key, number_of)
    heavy_load, usual = shares(number_of, rows * top, limit, lean, True), shares(number_of, rows * top, limit, lean, False)
    places = jnp.arange(number_of)

    def named(tallies, offset_by):
        used = int((tallies > 0).sum())
        fixed = max(1, used // 4)
        passed = fixed + (places - fixed + offset_by * (used - fixed)) % max(1, number_of - fixed)
        return jnp.zeros((number_of,), jnp.int32).at[sequence[jnp.where(places < fixed, places, passed)]].set(jnp.asarray(tallies, jnp.int32))

    tallies = jnp.where(number % 4 == 0, named(heavy_load, number // 4), named(usual, number - number // 4 - 1))
    mixed = jax.random.permutation(jax.random.fold_in(own, 3), number_of)
    source_of, taker = mixed[0:number_of // 2 * 2:2], mixed[1:number_of // 2 * 2:2]
    room = jnp.minimum(tallies[source_of] - 1, limit - tallies[taker]) // 2
    room = jnp.where((source_of == sequence[0]) | (taker == sequence[0]) | (tallies[taker] == 0), 0, jnp.maximum(room, 0))
    passed = jax.random.randint(jax.random.fold_in(own, 4), (number_of // 2,), 0, 1 << 20) % (room + 1)
    tallies = tallies.at[source_of].add(-passed).at[taker].add(passed)
    items = jnp.searchsorted(jnp.cumsum(tallies), jnp.arange(rows * top), side="right").astype(jnp.int32)
    listing = items.reshape(top, rows).T
    listing = listing[jax.random.permutation(jax.random.fold_in(own, 1), rows)]
    offset_by = jax.random.randint(jax.random.fold_in(own, 2), (rows, 1), 0, top)
    return jnp.take_along_axis(listing, (jnp.arange(top)[None, :] + offset_by) % top, axis=1)


def shares(amount, total, bound, slope, full):
    portions = [(1 << 20) // math.isqrt(grade ** slope) + 1 for grade in range(1, amount + 1)]
    largest = bound if full else min(bound, max(-(-total // amount), total * portions[0] // sum(portions)))
    least = 1 if total - largest >= amount - 1 else 0
    given, rest = [largest] + [least] * (amount - 1), total - largest - least * (amount - 1)
    while rest > 0:
        candidates = [i for i in range(1, amount) if given[i] < largest] or [i for i in range(1, amount) if given[i] < bound]
        whole, remaining = sum([portions[i] for i in candidates]), rest
        for i in candidates:
            extra = min(bound - given[i], max(1, remaining * portions[i] // whole), rest)
            given[i] = given[i] + extra
            rest = rest - extra
    return np.array(given)


def noise(own_key, extent, spread, reach, cuts=(), held_as=jnp.bfloat16):
    result = spread * jax.random.normal(own_key, extent, jnp.float32)
    if cuts:
        result = result * block_scale(own_key, extent, cuts, -0.22, 0.18)
    return jnp.clip(result, -reach, reach).astype(held_as)


def heavy_noise(key, extent, deviation, reach, cuts, heavy, held_as=jnp.bfloat16):
    drawn = deviation * jax.random.normal(key, extent, jnp.float32)
    if cuts:
        drawn = drawn * block_scale(key, extent, cuts, -0.22, 0.18)
    return jnp.clip(strengthened(drawn, jax.random.fold_in(key, 3), *heavy), -reach, reach).astype(held_as)


def setup_inputs(seed: int = 0) -> dict:
    arg_keys = jax.random.split(jax.random.key(seed), 14)
    layer_output_gradient = heavy_noise(arg_keys[0], (TOTAL_TOKENS, MODEL_DIM), 1.0, 24.0, ((0, 256),), (0, 1, 256, 6.0))
    residual_input = noise(arg_keys[1], (TOTAL_TOKENS, MODEL_DIM), 1.0, 6.0, ((0, 256),))
    norm_scale_vector = jnp.clip(1.0 + 0.1 * jax.random.normal(arg_keys[2], (MODEL_DIM,), jnp.float32), 0.5, 1.5).astype(jnp.bfloat16)
    chosen_expert_index_keys = jax.random.split(jax.random.fold_in(arg_keys[3], 1), TOTAL_TOKENS // GROUP)
    chosen_expert_index_turns = jax.random.permutation(jax.random.fold_in(arg_keys[3], 3), TOTAL_TOKENS // GROUP)
    chosen_expert_index = jax.vmap(lambda own, number: routed_block(jax.random.fold_in(arg_keys[3], 2), own, number, GROUP, EXPERTS, TOP, CAP, 2))(chosen_expert_index_keys, chosen_expert_index_turns).reshape((TOTAL_TOKENS, TOP))
    routing_gate_weight = jnp.clip(0.099609375 + 0.49804688 * jax.random.uniform(arg_keys[4], (TOTAL_TOKENS, TOP), jnp.float32) ** block_scale(arg_keys[4], (TOTAL_TOKENS, TOP), ((0, 256),), -0.2, 0.2), 0.099609375, 0.59765625).astype(jnp.bfloat16)
    expert_gate_weight = noise(arg_keys[5], (EXPERTS, MODEL_DIM, FF), MODEL_DIM ** -0.5, 0.0625, ((0, 64), (2, 4)))
    expert_up_weight = noise(arg_keys[6], (EXPERTS, MODEL_DIM, FF), MODEL_DIM ** -0.5, 0.0625, ((0, 64), (2, 4)))
    expert_down_weight = noise(arg_keys[7], (EXPERTS, FF, MODEL_DIM), FF ** -0.5, 0.1875, ((0, 64), (1, 4)))
    stored_gate_state = noise(arg_keys[8], (EXPERTS, SLOTS, FF), 1.5, 6.0, ((0, 64), (2, 4)))
    stored_up_state = noise(arg_keys[9], (EXPERTS, SLOTS, FF), 1.0, 6.0, ((0, 64), (2, 4)))
    attention_output = heavy_noise(arg_keys[10], (TOTAL_TOKENS, HEADS * VDIM), 1.0, 24.0, ((0, 256),), (0, 1, 256, 6.0))
    saved_adapter_latent = noise(arg_keys[11], (TOTAL_TOKENS, ADAPTER_RANK), ((9 * TOTAL_TOKENS) ** -0.5), 0.109375, ((0, 256),))
    adapter_up_matrix = noise(arg_keys[12], (ADAPTER_RANK, MODEL_DIM), (9 * MODEL_DIM * TOTAL_TOKENS) ** -0.5, 0.00048828125)
    return dict(layer_output_gradient=layer_output_gradient, residual_input=residual_input, norm_scale_vector=norm_scale_vector, chosen_expert_index=chosen_expert_index, routing_gate_weight=routing_gate_weight, expert_gate_weight=expert_gate_weight, expert_up_weight=expert_up_weight, expert_down_weight=expert_down_weight, stored_gate_state=stored_gate_state, stored_up_state=stored_up_state, attention_output=attention_output, saved_adapter_latent=saved_adapter_latent, adapter_up_matrix=adapter_up_matrix)


ADAPTER_SCALE = 2.0
NORM_EPS = 1e-06

def silu_parts(gate_val):
    sigmoid_val = jax.nn.sigmoid(gate_val)
    return (gate_val * sigmoid_val, sigmoid_val * (1.0 + gate_val * (1.0 - sigmoid_val)))

def slot_positions(chosen_expert_index):
    count = chosen_expert_index.shape[0]
    labels = jnp.arange(EXPERTS, dtype=jnp.int32)
    named_by = lax.optimization_barrier(jnp.sum((chosen_expert_index[:, :, None] == labels[None, None, :]).astype(jnp.int32), axis=1)).astype(jnp.int32)
    named_by = named_by.reshape(count // GROUP, GROUP, EXPERTS)
    before = (jnp.cumsum(named_by, axis=1) - named_by).astype(jnp.int32).reshape(count, EXPERTS)
    position = jnp.take_along_axis(before, chosen_expert_index, axis=1).astype(jnp.int32)
    block_of = (jnp.arange(count, dtype=jnp.int32) // GROUP)[:, None]
    return (block_of * CAP + position).astype(jnp.int32)

def reference(layer_output_gradient, residual_input, norm_scale_vector, chosen_expert_index, routing_gate_weight, expert_gate_weight, expert_up_weight, expert_down_weight, stored_gate_state, stored_up_state, attention_output, saved_adapter_latent, adapter_up_matrix):
    count = layer_output_gradient.shape[0]
    slot = slot_positions(chosen_expert_index)
    slot_index = (chosen_expert_index * SLOTS + slot).reshape(-1).astype(jnp.int32)
    token_ids = jnp.repeat(jnp.arange(count, dtype=jnp.int32), TOP)
    slot_owner = jnp.full((EXPERTS * SLOTS,), count, jnp.int32).at[slot_index].set(token_ids)
    slot_weight = jnp.zeros((EXPERTS * SLOTS,), jnp.float32).at[slot_index].set(routing_gate_weight.astype(jnp.float32).reshape(-1))
    slot_owner = slot_owner.reshape(EXPERTS, SLOTS)
    slot_weight = slot_weight.reshape(EXPERTS, SLOTS)
    padded = jnp.concatenate([layer_output_gradient, jnp.zeros((1, MODEL_DIM), layer_output_gradient.dtype)], axis=0)

    def one_expert(running, pieces):
        owner_row, weight_row, gate_mat, up_mat, down_mat, gate_saved, up_saved = pieces
        slot_rows = padded[owner_row]
        hidden_grad = jnp.dot(slot_rows, down_mat.T, preferred_element_type=jnp.float32)
        activation, silu_slope = silu_parts(gate_saved.astype(jnp.float32))
        gate_grad = (hidden_grad * up_saved.astype(jnp.float32) * silu_slope).astype(jnp.bfloat16)
        up_grad = (hidden_grad * activation).astype(jnp.bfloat16)
        merged = jnp.zeros((SLOTS, MODEL_DIM), jnp.float32)
        for quarter in range(N_SEQ):
            start = quarter * FF_DEV
            stop = start + FF_DEV
            partial_value = jnp.dot(gate_grad[:, start:stop], gate_mat[:, start:stop].T, preferred_element_type=jnp.float32)
            partial_value = partial_value + jnp.dot(up_grad[:, start:stop], up_mat[:, start:stop].T, preferred_element_type=jnp.float32)
            merged = merged + lax.optimization_barrier(partial_value.astype(jnp.bfloat16)).astype(jnp.float32)
        running = running.at[owner_row].add(merged * weight_row[:, None], mode='drop')
        return (running, None)
    moe_grad, _ = lax.scan(one_expert, jnp.zeros((count, MODEL_DIM), jnp.float32), (slot_owner, slot_weight, expert_gate_weight, expert_up_weight, expert_down_weight, stored_gate_state, stored_up_state))
    residual = residual_input.astype(jnp.float32)
    inverse_rms = lax.rsqrt(lax.optimization_barrier(jnp.mean(residual * residual, axis=1, keepdims=True)) + NORM_EPS)
    scaled = norm_scale_vector.astype(jnp.float32)[None, :] * moe_grad
    inner_mean = lax.optimization_barrier(jnp.mean(scaled * residual, axis=1, keepdims=True))
    hidden_state_gradient = (layer_output_gradient.astype(jnp.float32) + inverse_rms * scaled - residual * inner_mean * inverse_rms ** 3).astype(jnp.bfloat16)
    adapter_latent_value = (ADAPTER_SCALE * jnp.dot(hidden_state_gradient, adapter_up_matrix.T, preferred_element_type=jnp.float32)).astype(jnp.bfloat16)
    adapter_down_gradient = jnp.dot(attention_output.T, adapter_latent_value, preferred_element_type=jnp.float32)
    adapter_up_gradient_transposed = ADAPTER_SCALE * jnp.dot(hidden_state_gradient.T, saved_adapter_latent, preferred_element_type=jnp.float32)
    return (hidden_state_gradient, adapter_down_gradient, adapter_up_gradient_transposed)
```

```python
import jax
import jax.numpy as jnp
from jax import lax
from jax.sharding import PartitionSpec as P

ADAPTER_SCALE = 2.0
NORM_EPS = 1e-06
LANES = 128
CHUNKS = 2


def silu_parts(gate_val):
    sigmoid_val = jax.nn.sigmoid(gate_val)
    return (gate_val * sigmoid_val, sigmoid_val * (1.0 + gate_val * (1.0 - sigmoid_val)))


def contract_trailing(left, right):
    return lax.dot_general(
        left, right, (((1,), (1,)), ((), ())), preferred_element_type=jnp.float32
    )


def contract_leading(left, right):
    return lax.dot_general(
        left, right, (((0,), (0,)), ((), ())), preferred_element_type=jnp.float32
    )


def matmul(left, right):
    return lax.dot_general(
        left, right, (((1,), (0,)), ((), ())), preferred_element_type=jnp.float32
    )


def by_column(array, parts):
    rows, columns = array.shape
    return array.reshape(rows, parts, columns // parts).transpose(1, 0, 2)


def per_device(
    layer_output_gradient,
    residual_input,
    norm_scale_vector,
    chosen_expert_index,
    routing_gate_weight,
    expert_gate_weight,
    expert_up_weight,
    expert_down_weight,
    stored_gate_state,
    stored_up_state,
    attention_output,
    saved_adapter_latent,
    adapter_up_matrix,
):
    n_exp, n_seq = lax.axis_size("exp"), lax.axis_size("seq")
    my_exp, my_seq = lax.axis_index("exp"), lax.axis_index("seq")
    tokens, width = layer_output_gradient.shape
    top_count = chosen_expert_index.shape[1]
    rank = saved_adapter_latent.shape[1]
    experts = n_exp * expert_gate_weight.shape[0]
    capacity = stored_gate_state.shape[1] // experts
    heads_width = attention_output.shape[1]
    quarter, att_quarter = width // n_seq, heads_width // n_seq
    group = tokens * n_seq

    small = jnp.concatenate(
        [
            saved_adapter_latent,
            chosen_expert_index.astype(jnp.bfloat16),
            routing_gate_weight,
            jnp.zeros((tokens, LANES - rank - 2 * top_count), jnp.bfloat16),
        ],
        axis=1,
    )
    packed = jnp.concatenate(
        [
            by_column(layer_output_gradient, n_seq),
            by_column(residual_input, n_seq),
            by_column(attention_output, n_seq),
            jnp.broadcast_to(small[None], (n_seq, tokens, LANES)),
        ],
        axis=2,
    )
    packed = lax.all_to_all(packed, "seq", split_axis=0, concat_axis=0, tiled=True)
    packed = packed.reshape(group, -1)
    grad = packed[:, :quarter]
    residual = packed[:, quarter : 2 * quarter]
    attention = packed[:, 2 * quarter : 2 * quarter + att_quarter]
    small = packed[:, 2 * quarter + att_quarter :]
    latent = small[:, :rank]
    ids = small[:, rank : rank + top_count].astype(jnp.int32)
    weights = small[:, rank + top_count : rank + 2 * top_count].astype(jnp.float32)

    labels = jnp.arange(experts, dtype=jnp.int32)
    hits = (ids[:, :, None] == labels[None, None, :]).astype(jnp.float32)
    named = jnp.sum(hits, axis=1)
    named_weight = jnp.sum(hits * weights[:, :, None], axis=1)
    before = jnp.sum(
        jnp.where(
            jnp.arange(group)[:, None, None] > jnp.arange(group)[None, :, None], named[None], 0.0
        ),
        axis=1,
    )
    slot_of = jnp.where(named > 0.0, before.astype(jnp.int32), -1)
    taken = slot_of[:, :, None] == jnp.arange(capacity, dtype=jnp.int32)[None, None, :]
    taken = taken.reshape(group, experts * capacity)
    pick = taken.astype(jnp.bfloat16)
    spread = jnp.repeat(named_weight, capacity, axis=1)
    merge = jnp.where(taken, spread, 0.0).astype(jnp.bfloat16)

    piece = quarter // CHUNKS
    down = expert_down_weight[0]
    hidden_grad = None
    for chunk in range(CHUNKS):
        part = grad[:, chunk * piece : (chunk + 1) * piece]
        outgoing = contract_leading(pick, part).astype(jnp.bfloat16)
        outgoing = outgoing.reshape(experts, capacity, piece)
        incoming = lax.all_to_all(outgoing, "exp", split_axis=0, concat_axis=0, tiled=True)
        rows = lax.all_gather(incoming.reshape(-1, piece), "seq", axis=0)
        for source in range(n_seq):
            first = source * quarter + chunk * piece
            term = contract_trailing(rows[source], down[:, first : first + piece])
            hidden_grad = term if hidden_grad is None else hidden_grad + term

    activation, silu_slope = silu_parts(stored_gate_state[0].astype(jnp.float32))
    gate_grad = (hidden_grad * stored_up_state[0].astype(jnp.float32) * silu_slope).astype(
        jnp.bfloat16
    )
    up_grad = (hidden_grad * activation).astype(jnp.bfloat16)

    moe_parts = []
    for chunk in range(CHUNKS):
        pieces = []
        for source in range(n_seq):
            first = source * quarter + chunk * piece
            value = contract_trailing(
                gate_grad, expert_gate_weight[0, first : first + piece]
            ) + contract_trailing(up_grad, expert_up_weight[0, first : first + piece])
            pieces.append(value.astype(jnp.bfloat16))
        summed = lax.psum_scatter(jnp.stack(pieces), "seq", scatter_dimension=0, tiled=False)
        returned = lax.all_to_all(
            summed.reshape(experts, capacity, piece),
            "exp",
            split_axis=0,
            concat_axis=0,
            tiled=True,
        )
        moe_parts.append(matmul(merge, returned.reshape(experts * capacity, piece)))
    moe_grad = jnp.concatenate(moe_parts, axis=1)

    residual = residual.astype(jnp.float32)
    grad = grad.astype(jnp.float32)
    scale = lax.dynamic_slice_in_dim(norm_scale_vector, my_seq * quarter, quarter, 0)
    adapter = lax.dynamic_slice_in_dim(adapter_up_matrix, my_seq * quarter, quarter, 1)
    square_sum = lax.psum(jnp.sum(residual * residual, axis=1, keepdims=True), "seq")
    inverse_rms = lax.rsqrt(square_sum / width + NORM_EPS)
    scaled = scale.astype(jnp.float32)[None, :] * moe_grad
    inner_mean = lax.psum(jnp.sum(scaled * residual, axis=1, keepdims=True), "seq") / width
    hidden_state = (
        grad + inverse_rms * scaled - residual * inner_mean * inverse_rms**3
    ).astype(jnp.bfloat16)
    act = ADAPTER_SCALE * lax.psum(contract_trailing(hidden_state, adapter), "seq")
    act = act.astype(jnp.bfloat16)
    down_rows = contract_leading(attention, act).reshape(n_exp, att_quarter // n_exp, rank)
    up_rows = ADAPTER_SCALE * contract_leading(hidden_state, latent).reshape(
        n_exp, quarter // n_exp, rank
    )
    total = lax.psum_scatter(
        jnp.concatenate([down_rows, up_rows], axis=1), "exp", scatter_dimension=0, tiled=False
    )
    members = n_exp * n_seq
    route = [
        (member, (member % n_seq) * n_exp + member // n_seq) for member in range(members)
    ]
    total = lax.ppermute(total, ("exp", "seq"), route)
    hidden_rows = lax.all_to_all(
        hidden_state.reshape(n_seq, tokens, quarter),
        "seq",
        split_axis=0,
        concat_axis=0,
        tiled=True,
    )
    hidden_rows = hidden_rows.transpose(1, 0, 2).reshape(tokens, width)
    return (
        hidden_rows,
        total[: att_quarter // n_exp],
        total[att_quarter // n_exp :],
    )


def solution(mesh):
    return jax.shard_map(
        per_device,
        mesh=mesh,
        in_specs=(
            P(("exp", "seq"), None),
            P(("exp", "seq"), None),
            P(),
            P(("exp", "seq"), None),
            P(("exp", "seq"), None),
            P("exp", None, "seq"),
            P("exp", None, "seq"),
            P("exp", "seq", None),
            P("exp", None, "seq"),
            P("exp", None, "seq"),
            P(("exp", "seq"), None),
            P(("exp", "seq"), None),
            P(),
        ),
        out_specs=(P(("exp", "seq"), None), P(("exp", "seq"), None), P(("exp", "seq"), None)),
        check_vma=False,
    )
```

```python
import jax
import jax.numpy as jnp
from jax import lax
from jax.sharding import PartitionSpec as P

ADAPTER_SCALE = 2.0
NORM_EPS = 1e-06
LANES = 128
OUT_TILES = (3, 5, 6)
BACK_TILES = (6, 5, 3)


def silu_parts(gate_val):
    sigmoid_val = jax.nn.sigmoid(gate_val)
    return (gate_val * sigmoid_val, sigmoid_val * (1.0 + gate_val * (1.0 - sigmoid_val)))


def contract_trailing(left, right):
    return lax.dot_general(
        left, right, (((1,), (1,)), ((), ())), preferred_element_type=jnp.float32
    )


def contract_leading(left, right):
    return lax.dot_general(
        left, right, (((0,), (0,)), ((), ())), preferred_element_type=jnp.float32
    )


def matmul(left, right):
    return lax.dot_general(
        left, right, (((1,), (0,)), ((), ())), preferred_element_type=jnp.float32
    )


def by_column(array, parts):
    rows, columns = array.shape
    return array.reshape(rows, parts, columns // parts).transpose(1, 0, 2)


def per_device(
    layer_output_gradient,
    residual_input,
    norm_scale_vector,
    chosen_expert_index,
    routing_gate_weight,
    expert_gate_weight,
    expert_up_weight,
    expert_down_weight,
    stored_gate_state,
    stored_up_state,
    attention_output,
    saved_adapter_latent,
    adapter_up_matrix,
):
    n_exp, n_seq = lax.axis_size("exp"), lax.axis_size("seq")
    my_seq = lax.axis_index("seq")
    tokens, width = layer_output_gradient.shape
    top_count = chosen_expert_index.shape[1]
    rank = saved_adapter_latent.shape[1]
    experts = n_exp * expert_gate_weight.shape[0]
    capacity = stored_gate_state.shape[1] // experts
    heads_width = attention_output.shape[1]
    quarter, att_quarter = width // n_seq, heads_width // n_seq
    group = tokens * n_seq

    small = jnp.concatenate(
        [
            saved_adapter_latent,
            chosen_expert_index.astype(jnp.bfloat16),
            routing_gate_weight,
            jnp.zeros((tokens, LANES - rank - 2 * top_count), jnp.bfloat16),
        ],
        axis=1,
    )
    packed = jnp.concatenate(
        [
            by_column(layer_output_gradient, n_seq),
            by_column(residual_input, n_seq),
            by_column(attention_output, n_seq),
            jnp.broadcast_to(small[None], (n_seq, tokens, LANES)),
        ],
        axis=2,
    )
    packed = lax.all_to_all(packed, "seq", split_axis=0, concat_axis=0, tiled=True)
    packed = packed.reshape(group, -1)
    grad = packed[:, :quarter]
    residual = packed[:, quarter : 2 * quarter]
    attention = packed[:, 2 * quarter : 2 * quarter + att_quarter]
    small = packed[:, 2 * quarter + att_quarter :]
    latent = small[:, :rank]
    ids = small[:, rank : rank + top_count].astype(jnp.int32)
    weights = small[:, rank + top_count : rank + 2 * top_count].astype(jnp.float32)

    labels = jnp.arange(experts, dtype=jnp.int32)
    hits = (ids[:, :, None] == labels[None, None, :]).astype(jnp.float32)
    named = jnp.sum(hits, axis=1)
    named_weight = jnp.sum(hits * weights[:, :, None], axis=1)
    before = jnp.sum(
        jnp.where(
            jnp.arange(group)[:, None, None] > jnp.arange(group)[None, :, None], named[None], 0.0
        ),
        axis=1,
    )
    slot_of = jnp.where(named > 0.0, before.astype(jnp.int32), -1)
    taken = slot_of[:, :, None] == jnp.arange(capacity, dtype=jnp.int32)[None, None, :]
    taken = taken.reshape(group, experts * capacity)
    pick = taken.astype(jnp.bfloat16)
    spread = jnp.repeat(named_weight, capacity, axis=1)
    merge = jnp.where(taken, spread, 0.0).astype(jnp.bfloat16)

    att_piece, hid_piece = att_quarter // n_exp, quarter // n_exp
    lora_left = jnp.concatenate(
        [
            attention.reshape(group, n_exp, att_piece),
            jnp.broadcast_to(latent[:, None], (group, n_exp, rank)),
            jnp.zeros((group, n_exp, LANES - att_piece - rank), jnp.bfloat16),
        ],
        axis=2,
    ).transpose(1, 0, 2)

    down = expert_down_weight[0]
    hidden_grad = None
    start = 0
    for index, tiles in enumerate(OUT_TILES):
        piece = tiles * LANES
        outgoing = contract_leading(pick, grad[:, start : start + piece]).astype(jnp.bfloat16)
        outgoing = outgoing.reshape(experts, capacity, piece)
        incoming = lax.all_to_all(outgoing, "exp", split_axis=0, concat_axis=0, tiled=True)
        last = index == len(OUT_TILES) - 1
        if last:
            incoming, lora_left = lax.optimization_barrier((incoming, lora_left))
        rows = lax.all_gather(incoming.reshape(-1, piece), "seq", axis=0)
        if last:
            lora_left = lax.all_to_all(lora_left, "exp", split_axis=0, concat_axis=0, tiled=True)
            rows, lora_left = lax.optimization_barrier((rows, lora_left))
        for source in range(n_seq):
            first = source * quarter + start
            term = contract_trailing(rows[source], down[:, first : first + piece])
            hidden_grad = term if hidden_grad is None else hidden_grad + term
        start += piece

    activation, silu_slope = silu_parts(stored_gate_state[0].astype(jnp.float32))
    gate_grad = (hidden_grad * stored_up_state[0].astype(jnp.float32) * silu_slope).astype(
        jnp.bfloat16
    )
    up_grad = (hidden_grad * activation).astype(jnp.bfloat16)

    returned = []

    def send_back(summed):
        returned.append(
            lax.all_to_all(
                summed.reshape(experts, capacity, -1),
                "exp",
                split_axis=0,
                concat_axis=0,
                tiled=True,
            )
        )

    start, summed = 0, None
    for tiles in BACK_TILES:
        piece = tiles * LANES
        pieces = []
        for source in range(n_seq):
            first = source * quarter + start
            value = contract_trailing(
                gate_grad, expert_gate_weight[0, first : first + piece]
            ) + contract_trailing(up_grad, expert_up_weight[0, first : first + piece])
            pieces.append(value.astype(jnp.bfloat16))
        partial_value = jnp.stack(pieces)
        if summed is not None:
            partial_value, summed, returned = lax.optimization_barrier(
                (partial_value, summed, returned)
            )
        following = lax.psum_scatter(partial_value, "seq", scatter_dimension=0, tiled=False)
        if summed is not None:
            send_back(summed)
        start, summed = start + piece, following
    send_back(summed)
    moe_parts = [
        matmul(merge, block.reshape(experts * capacity, -1)) for block in returned
    ]
    moe_grad = jnp.concatenate(moe_parts, axis=1)

    scale = lax.dynamic_slice_in_dim(norm_scale_vector, my_seq * quarter, quarter, 0)
    adapter = lax.dynamic_slice_in_dim(adapter_up_matrix, my_seq * quarter, quarter, 1)
    residual_f32 = residual.astype(jnp.float32)
    scaled = scale.astype(jnp.float32)[None, :] * moe_grad
    sums = jnp.concatenate(
        [
            contract_trailing(grad, adapter),
            contract_trailing(residual, adapter),
            contract_trailing(scaled.astype(jnp.bfloat16), adapter),
            jnp.sum(residual_f32 * residual_f32, axis=1, keepdims=True),
            jnp.sum(scaled * residual_f32, axis=1, keepdims=True),
            jnp.zeros((group, LANES - 3 * rank - 2), jnp.float32),
        ],
        axis=1,
    )
    sums = lax.psum(sums, "seq")
    inverse_rms = lax.rsqrt(sums[:, 3 * rank : 3 * rank + 1] / width + NORM_EPS)
    back = sums[:, 3 * rank + 1 : 3 * rank + 2] / width * inverse_rms**3
    hidden_state = (
        grad.astype(jnp.float32) + inverse_rms * scaled - residual_f32 * back
    ).astype(jnp.bfloat16)
    act = ADAPTER_SCALE * (
        sums[:, :rank]
        + inverse_rms * sums[:, 2 * rank : 3 * rank]
        - back * sums[:, rank : 2 * rank]
    )
    act = act.astype(jnp.bfloat16)
    lora_right = jnp.concatenate(
        [
            hidden_state.reshape(group, n_exp, hid_piece),
            jnp.zeros((group, n_exp, att_piece - hid_piece), jnp.bfloat16),
            jnp.broadcast_to(act[:, None], (group, n_exp, rank)),
            jnp.zeros((group, n_exp, LANES - att_piece - rank), jnp.bfloat16),
        ],
        axis=2,
    ).transpose(1, 0, 2)
    lora_right = lax.all_to_all(lora_right, "exp", split_axis=0, concat_axis=0, tiled=True)
    products = contract_leading(
        lora_left.reshape(-1, LANES), lora_right.reshape(-1, LANES)
    )
    down_rows = products[:att_piece, att_piece : att_piece + rank]
    up_rows = ADAPTER_SCALE * products[att_piece : att_piece + rank, :hid_piece].T
    total = jnp.concatenate([down_rows, up_rows], axis=0)
    members = n_exp * n_seq
    route = [
        (member, (member % n_seq) * n_exp + member // n_seq) for member in range(members)
    ]
    total = lax.ppermute(total, ("exp", "seq"), route)
    hidden_rows = lax.all_to_all(
        hidden_state.reshape(n_seq, tokens, quarter),
        "seq",
        split_axis=0,
        concat_axis=0,
        tiled=True,
    )
    hidden_rows = hidden_rows.transpose(1, 0, 2).reshape(tokens, width)
    return (
        hidden_rows,
        total[:att_piece],
        total[att_piece:],
    )


def solution(mesh):
    return jax.shard_map(
        per_device,
        mesh=mesh,
        in_specs=(
            P(("exp", "seq"), None),
            P(("exp", "seq"), None),
            P(),
            P(("exp", "seq"), None),
            P(("exp", "seq"), None),
            P("exp", None, "seq"),
            P("exp", None, "seq"),
            P("exp", "seq", None),
            P("exp", None, "seq"),
            P("exp", None, "seq"),
            P(("exp", "seq"), None),
            P(("exp", "seq"), None),
            P(),
        ),
        out_specs=(P(("exp", "seq"), None), P(("exp", "seq"), None), P(("exp", "seq"), None)),
        check_vma=False,
    )
```

```python
import jax
import jax.numpy as jnp
from jax import lax
from jax.sharding import PartitionSpec as P

ADAPTER_SCALE = 2.0
NORM_EPS = 1e-06
LANES = 128
OUT_TILES = (6, 8)
BACK_TILES = (8, 6)


def silu_parts(gate_val):
    sigmoid_val = jax.nn.sigmoid(gate_val)
    return (gate_val * sigmoid_val, sigmoid_val * (1.0 + gate_val * (1.0 - sigmoid_val)))


def contract_trailing(left, right):
    return lax.dot_general(
        left, right, (((1,), (1,)), ((), ())), preferred_element_type=jnp.float32
    )


def contract_leading(left, right):
    return lax.dot_general(
        left, right, (((0,), (0,)), ((), ())), preferred_element_type=jnp.float32
    )


def matmul(left, right):
    return lax.dot_general(
        left, right, (((1,), (0,)), ((), ())), preferred_element_type=jnp.float32
    )


def by_column(array, parts):
    rows, columns = array.shape
    return array.reshape(rows, parts, columns // parts).transpose(1, 0, 2)


def per_device(
    layer_output_gradient,
    residual_input,
    norm_scale_vector,
    chosen_expert_index,
    routing_gate_weight,
    expert_gate_weight,
    expert_up_weight,
    expert_down_weight,
    stored_gate_state,
    stored_up_state,
    attention_output,
    saved_adapter_latent,
    adapter_up_matrix,
):
    n_exp, n_seq = lax.axis_size("exp"), lax.axis_size("seq")
    my_seq = lax.axis_index("seq")
    tokens, width = layer_output_gradient.shape
    top_count = chosen_expert_index.shape[1]
    rank = saved_adapter_latent.shape[1]
    experts = n_exp * expert_gate_weight.shape[0]
    capacity = stored_gate_state.shape[1] // experts
    heads_width = attention_output.shape[1]
    quarter, att_quarter = width // n_seq, heads_width // n_seq
    group = tokens * n_seq

    small = jnp.concatenate(
        [
            saved_adapter_latent,
            chosen_expert_index.astype(jnp.bfloat16),
            routing_gate_weight,
            jnp.zeros((tokens, LANES - rank - 2 * top_count), jnp.bfloat16),
        ],
        axis=1,
    )
    packed = jnp.concatenate(
        [
            by_column(layer_output_gradient, n_seq),
            by_column(residual_input, n_seq),
            by_column(attention_output, n_seq),
            jnp.broadcast_to(small[None], (n_seq, tokens, LANES)),
        ],
        axis=2,
    )
    packed = lax.all_to_all(packed, "seq", split_axis=0, concat_axis=0, tiled=True)
    packed = packed.reshape(group, -1)
    grad = packed[:, :quarter]
    residual = packed[:, quarter : 2 * quarter]
    attention = packed[:, 2 * quarter : 2 * quarter + att_quarter]
    small = packed[:, 2 * quarter + att_quarter :]
    latent = small[:, :rank]
    ids = small[:, rank : rank + top_count].astype(jnp.int32)
    weights = small[:, rank + top_count : rank + 2 * top_count].astype(jnp.float32)

    labels = jnp.arange(experts, dtype=jnp.int32)
    hits = (ids[:, :, None] == labels[None, None, :]).astype(jnp.float32)
    named = jnp.sum(hits, axis=1)
    named_weight = jnp.sum(hits * weights[:, :, None], axis=1)
    before = jnp.sum(
        jnp.where(
            jnp.arange(group)[:, None, None] > jnp.arange(group)[None, :, None], named[None], 0.0
        ),
        axis=1,
    )
    slot_of = jnp.where(named > 0.0, before.astype(jnp.int32), -1)
    taken = slot_of[:, :, None] == jnp.arange(capacity, dtype=jnp.int32)[None, None, :]
    taken = taken.reshape(group, experts * capacity)
    pick = taken.astype(jnp.bfloat16)
    spread = jnp.repeat(named_weight, capacity, axis=1)
    merge = jnp.where(taken, spread, 0.0).astype(jnp.bfloat16)

    att_piece, hid_piece = att_quarter // n_exp, quarter // n_exp
    lora_left = jnp.concatenate(
        [
            attention.reshape(group, n_exp, att_piece),
            jnp.broadcast_to(latent[:, None], (group, n_exp, rank)),
            jnp.zeros((group, n_exp, LANES - att_piece - rank), jnp.bfloat16),
        ],
        axis=2,
    ).transpose(1, 0, 2)

    down = expert_down_weight[0]
    hidden_grad = None
    start = 0
    for index, tiles in enumerate(OUT_TILES):
        piece = tiles * LANES
        outgoing = contract_leading(pick, grad[:, start : start + piece]).astype(jnp.bfloat16)
        outgoing = outgoing.reshape(experts, capacity, piece)
        incoming = lax.all_to_all(outgoing, "exp", split_axis=0, concat_axis=0, tiled=True)
        last = index == len(OUT_TILES) - 1
        if last:
            incoming, lora_left = lax.optimization_barrier((incoming, lora_left))
        rows = lax.all_gather(incoming.reshape(-1, piece), "seq", axis=0)
        if last:
            lora_left = lax.all_to_all(lora_left, "exp", split_axis=0, concat_axis=0, tiled=True)
            rows, lora_left = lax.optimization_barrier((rows, lora_left))
        for source in range(n_seq):
            first = source * quarter + start
            term = contract_trailing(rows[source], down[:, first : first + piece])
            hidden_grad = term if hidden_grad is None else hidden_grad + term
        start += piece

    activation, silu_slope = silu_parts(stored_gate_state[0].astype(jnp.float32))
    gate_grad = (hidden_grad * stored_up_state[0].astype(jnp.float32) * silu_slope).astype(
        jnp.bfloat16
    )
    up_grad = (hidden_grad * activation).astype(jnp.bfloat16)

    returned = []

    def send_back(summed):
        returned.append(
            lax.all_to_all(
                summed.reshape(experts, capacity, -1),
                "exp",
                split_axis=0,
                concat_axis=0,
                tiled=True,
            )
        )

    start, summed = 0, None
    for tiles in BACK_TILES:
        piece = tiles * LANES
        pieces = []
        for source in range(n_seq):
            first = source * quarter + start
            value = contract_trailing(
                gate_grad, expert_gate_weight[0, first : first + piece]
            ) + contract_trailing(up_grad, expert_up_weight[0, first : first + piece])
            pieces.append(value.astype(jnp.bfloat16))
        partial_value = jnp.stack(pieces)
        if summed is not None:
            partial_value, summed, returned = lax.optimization_barrier(
                (partial_value, summed, returned)
            )
        following = lax.psum_scatter(partial_value, "seq", scatter_dimension=0, tiled=False)
        if summed is not None:
            send_back(summed)
        start, summed = start + piece, following
    send_back(summed)
    moe_parts = [
        matmul(merge, block.reshape(experts * capacity, -1)) for block in returned
    ]
    moe_grad = jnp.concatenate(moe_parts, axis=1)

    scale = lax.dynamic_slice_in_dim(norm_scale_vector, my_seq * quarter, quarter, 0)
    adapter = lax.dynamic_slice_in_dim(adapter_up_matrix, my_seq * quarter, quarter, 1)
    residual_f32 = residual.astype(jnp.float32)
    scaled = scale.astype(jnp.float32)[None, :] * moe_grad
    sums = jnp.concatenate(
        [
            contract_trailing(grad, adapter),
            contract_trailing(residual, adapter),
            contract_trailing(scaled.astype(jnp.bfloat16), adapter),
            jnp.sum(residual_f32 * residual_f32, axis=1, keepdims=True),
            jnp.sum(scaled * residual_f32, axis=1, keepdims=True),
            jnp.zeros((group, LANES - 3 * rank - 2), jnp.float32),
        ],
        axis=1,
    )
    sums = lax.psum(sums, "seq")
    inverse_rms = lax.rsqrt(sums[:, 3 * rank : 3 * rank + 1] / width + NORM_EPS)
    back = sums[:, 3 * rank + 1 : 3 * rank + 2] / width * inverse_rms**3
    hidden_state = (
        grad.astype(jnp.float32) + inverse_rms * scaled - residual_f32 * back
    ).astype(jnp.bfloat16)
    act = ADAPTER_SCALE * (
        sums[:, :rank]
        + inverse_rms * sums[:, 2 * rank : 3 * rank]
        - back * sums[:, rank : 2 * rank]
    )
    act = act.astype(jnp.bfloat16)
    lora_right = jnp.concatenate(
        [
            hidden_state.reshape(group, n_exp, hid_piece),
            jnp.zeros((group, n_exp, att_piece - hid_piece), jnp.bfloat16),
            jnp.broadcast_to(act[:, None], (group, n_exp, rank)),
            jnp.zeros((group, n_exp, LANES - att_piece - rank), jnp.bfloat16),
        ],
        axis=2,
    ).transpose(1, 0, 2)
    lora_right = lax.all_to_all(lora_right, "exp", split_axis=0, concat_axis=0, tiled=True)
    products = contract_leading(
        lora_left.reshape(-1, LANES), lora_right.reshape(-1, LANES)
    )
    down_rows = products[:att_piece, att_piece : att_piece + rank]
    up_rows = ADAPTER_SCALE * products[att_piece : att_piece + rank, :hid_piece].T
    total = jnp.concatenate([down_rows, up_rows], axis=0)
    members = n_exp * n_seq
    route = [
        (member, (member % n_seq) * n_exp + member // n_seq) for member in range(members)
    ]
    total = lax.ppermute(total, ("exp", "seq"), route)
    hidden_rows = lax.all_to_all(
        hidden_state.reshape(n_seq, tokens, quarter),
        "seq",
        split_axis=0,
        concat_axis=0,
        tiled=True,
    )
    hidden_rows = hidden_rows.transpose(1, 0, 2).reshape(tokens, width)
    return (
        hidden_rows,
        total[:att_piece],
        total[att_piece:],
    )


def solution(mesh):
    return jax.shard_map(
        per_device,
        mesh=mesh,
        in_specs=(
            P(("exp", "seq"), None),
            P(("exp", "seq"), None),
            P(),
            P(("exp", "seq"), None),
            P(("exp", "seq"), None),
            P("exp", None, "seq"),
            P("exp", None, "seq"),
            P("exp", "seq", None),
            P("exp", None, "seq"),
            P("exp", None, "seq"),
            P(("exp", "seq"), None),
            P(("exp", "seq"), None),
            P(),
        ),
        out_specs=(P(("exp", "seq"), None), P(("exp", "seq"), None), P(("exp", "seq"), None)),
        check_vma=False,
    )
```

```python
import functools

import jax
import jax.numpy as jnp
from jax import lax
from jax.experimental import pallas as pl
from jax.experimental.pallas import tpu as pltpu
from jax.sharding import PartitionSpec as P

ADAPTER_SCALE = 2.0
NORM_EPS = 1e-06
LANES = 128
BACK_TILES = (8, 6)
MESH = pl.DeviceIdType.MESH


def silu_parts(gate_val):
    sigmoid_val = jax.nn.sigmoid(gate_val)
    return (gate_val * sigmoid_val, sigmoid_val * (1.0 + gate_val * (1.0 - sigmoid_val)))


def contract_trailing(left, right):
    return lax.dot_general(
        left, right, (((1,), (1,)), ((), ())), preferred_element_type=jnp.float32
    )


def contract_leading(left, right):
    return lax.dot_general(
        left, right, (((0,), (0,)), ((), ())), preferred_element_type=jnp.float32
    )


def matmul(left, right):
    return lax.dot_general(
        left, right, (((1,), (0,)), ((), ())), preferred_element_type=jnp.float32
    )


def by_column(array, parts):
    rows, columns = array.shape
    return array.reshape(rows, parts, columns // parts).transpose(1, 0, 2)


def dispatch_kernel(
    n_exp, n_seq, outgoing, rows, own_sem, send_sem, recv_sem, side_send, right_sem, left_sem,
    far_send, far_sem,
):
    me, seq = lax.axis_index("exp"), lax.axis_index("seq")
    right, left = lax.rem(seq + 1, n_seq), lax.rem(seq + n_seq - 1, n_seq)

    barrier = pltpu.get_barrier_semaphore()

    def greet(offset, carry):
        pl.semaphore_signal(
            barrier, inc=1, device_id=(lax.rem(me + offset, n_exp), seq), device_id_type=MESH
        )
        return carry

    lax.fori_loop(1, n_exp, greet, 0)
    for other in (right, left):
        pl.semaphore_signal(barrier, inc=1, device_id=(me, other), device_id_type=MESH)
    pl.semaphore_wait(barrier, n_exp + 1)

    own = pltpu.make_async_copy(outgoing.at[me], rows.at[seq, me], own_sem)
    own.start()

    def over_exp(offset):
        other = lax.rem(me + offset, n_exp)
        return pltpu.make_async_remote_copy(
            src_ref=outgoing.at[other],
            dst_ref=rows.at[seq, me],
            send_sem=send_sem.at[offset],
            recv_sem=recv_sem.at[offset],
            device_id=(other, seq),
            device_id_type=MESH,
        )

    def start_over_exp(offset, carry):
        over_exp(offset).start()
        return carry

    lax.fori_loop(1, n_exp, start_over_exp, 0)
    own.wait()

    def beside(offset, towards, columns, send, recv):
        block = rows.at[columns, lax.rem(me - offset + n_exp, n_exp)]
        return pltpu.make_async_remote_copy(
            src_ref=block,
            dst_ref=block,
            send_sem=send,
            recv_sem=recv,
            device_id=(me, towards),
            device_id_type=MESH,
        )

    def to_right(offset):
        return beside(offset, right, seq, side_send.at[0, offset], right_sem.at[offset])

    def to_left(offset):
        return beside(offset, left, seq, side_send.at[1, offset], left_sem.at[offset])

    def onward_right(offset):
        return beside(offset, right, left, far_send.at[offset], far_sem.at[offset])

    def onward_left(offset):
        return beside(offset, left, right, far_send.at[offset], far_sem.at[offset])

    def spread(offset):
        to_right(offset).start()
        to_left(offset).start()

    def onward(pair):
        to_right(2 * pair).wait_recv()
        onward_right(2 * pair).start()
        to_left(2 * pair).wait_recv()
        to_right(2 * pair + 1).wait_recv()
        to_left(2 * pair + 1).wait_recv()
        onward_left(2 * pair + 1).start()

    def arrive(offset):
        over_exp(offset).wait_recv()
        spread(offset)

    spread(0)
    arrive(1)

    def step(pair, carry):
        arrive(2 * pair)
        arrive(2 * pair + 1)
        onward(pair - 1)
        return carry

    lax.fori_loop(1, n_exp // 2, step, 0)
    onward(n_exp // 2 - 1)

    def finish(pair, carry):
        for offset in (2 * pair, 2 * pair + 1):
            to_right(offset).wait_send()
            to_left(offset).wait_send()
        onward_right(2 * pair).wait()
        onward_left(2 * pair + 1).wait()
        return carry

    lax.fori_loop(0, n_exp // 2, finish, 0)

    def sent(offset, carry):
        over_exp(offset).wait_send()
        return carry

    lax.fori_loop(1, n_exp, sent, 0)


def dispatch(outgoing, n_exp, n_seq):
    return pl.pallas_call(
        functools.partial(dispatch_kernel, n_exp, n_seq),
        out_shape=jax.ShapeDtypeStruct((n_seq,) + outgoing.shape, outgoing.dtype),
        in_specs=[pl.BlockSpec(memory_space=pl.ANY)],
        out_specs=pl.BlockSpec(memory_space=pl.ANY),
        scratch_shapes=[
            pltpu.SemaphoreType.DMA,
            pltpu.SemaphoreType.DMA((n_exp,)),
            pltpu.SemaphoreType.DMA((n_exp,)),
            pltpu.SemaphoreType.DMA((2, n_exp)),
            pltpu.SemaphoreType.DMA((n_exp,)),
            pltpu.SemaphoreType.DMA((n_exp,)),
            pltpu.SemaphoreType.DMA((n_exp,)),
            pltpu.SemaphoreType.DMA((n_exp,)),
        ],
        compiler_params=pltpu.CompilerParams(
            collective_id=0, has_side_effects=True, vmem_limit_bytes=1 << 20
        ),
    )(outgoing)


def per_device(
    layer_output_gradient,
    residual_input,
    norm_scale_vector,
    chosen_expert_index,
    routing_gate_weight,
    expert_gate_weight,
    expert_up_weight,
    expert_down_weight,
    stored_gate_state,
    stored_up_state,
    attention_output,
    saved_adapter_latent,
    adapter_up_matrix,
):
    n_exp, n_seq = lax.axis_size("exp"), lax.axis_size("seq")
    my_seq = lax.axis_index("seq")
    tokens, width = layer_output_gradient.shape
    top_count = chosen_expert_index.shape[1]
    rank = saved_adapter_latent.shape[1]
    experts = n_exp * expert_gate_weight.shape[0]
    capacity = stored_gate_state.shape[1] // experts
    heads_width = attention_output.shape[1]
    quarter, att_quarter = width // n_seq, heads_width // n_seq
    group = tokens * n_seq

    small = jnp.concatenate(
        [
            saved_adapter_latent,
            chosen_expert_index.astype(jnp.bfloat16),
            routing_gate_weight,
            jnp.zeros((tokens, LANES - rank - 2 * top_count), jnp.bfloat16),
        ],
        axis=1,
    )
    packed = jnp.concatenate(
        [
            by_column(layer_output_gradient, n_seq),
            by_column(residual_input, n_seq),
            by_column(attention_output, n_seq),
            jnp.broadcast_to(small[None], (n_seq, tokens, LANES)),
        ],
        axis=2,
    )
    packed = lax.all_to_all(packed, "seq", split_axis=0, concat_axis=0, tiled=True)
    packed = packed.reshape(group, -1)
    grad = packed[:, :quarter]
    residual = packed[:, quarter : 2 * quarter]
    attention = packed[:, 2 * quarter : 2 * quarter + att_quarter]
    small = packed[:, 2 * quarter + att_quarter :]
    latent = small[:, :rank]
    ids = small[:, rank : rank + top_count].astype(jnp.int32)
    weights = small[:, rank + top_count : rank + 2 * top_count].astype(jnp.float32)

    labels = jnp.arange(experts, dtype=jnp.int32)
    hits = (ids[:, :, None] == labels[None, None, :]).astype(jnp.float32)
    named = jnp.sum(hits, axis=1)
    named_weight = jnp.sum(hits * weights[:, :, None], axis=1)
    before = jnp.sum(
        jnp.where(
            jnp.arange(group)[:, None, None] > jnp.arange(group)[None, :, None], named[None], 0.0
        ),
        axis=1,
    )
    slot_of = jnp.where(named > 0.0, before.astype(jnp.int32), -1)
    taken = slot_of[:, :, None] == jnp.arange(capacity, dtype=jnp.int32)[None, None, :]
    taken = taken.reshape(group, experts * capacity)
    pick = taken.astype(jnp.bfloat16)
    spread = jnp.repeat(named_weight, capacity, axis=1)
    merge = jnp.where(taken, spread, 0.0).astype(jnp.bfloat16)

    att_piece, hid_piece = att_quarter // n_exp, quarter // n_exp
    lora_left = jnp.concatenate(
        [
            attention.reshape(group, n_exp, att_piece),
            jnp.broadcast_to(latent[:, None], (group, n_exp, rank)),
            jnp.zeros((group, n_exp, LANES - att_piece - rank), jnp.bfloat16),
        ],
        axis=2,
    ).transpose(1, 0, 2)

    down = expert_down_weight[0]
    outgoing = contract_leading(pick, grad).astype(jnp.bfloat16)
    rows = dispatch(outgoing.reshape(experts, capacity, quarter), n_exp, n_seq)
    rows = rows.reshape(n_seq, -1, quarter)
    hidden_grad = None
    for source in range(n_seq):
        term = contract_trailing(rows[source], down[:, source * quarter : (source + 1) * quarter])
        hidden_grad = term if hidden_grad is None else hidden_grad + term
    activation, silu_slope = silu_parts(stored_gate_state[0].astype(jnp.float32))
    gate_grad = (hidden_grad * stored_up_state[0].astype(jnp.float32) * silu_slope).astype(
        jnp.bfloat16
    )
    up_grad = (hidden_grad * activation).astype(jnp.bfloat16)

    returned = []

    def send_back(summed):
        returned.append(
            lax.all_to_all(
                summed.reshape(experts, capacity, -1),
                "exp",
                split_axis=0,
                concat_axis=0,
                tiled=True,
            )
        )

    start, summed = 0, None
    for tiles in BACK_TILES:
        piece = tiles * LANES
        pieces = []
        for source in range(n_seq):
            first = source * quarter + start
            value = contract_trailing(
                gate_grad, expert_gate_weight[0, first : first + piece]
            ) + contract_trailing(up_grad, expert_up_weight[0, first : first + piece])
            pieces.append(value.astype(jnp.bfloat16))
        partial_value = jnp.stack(pieces)
        if summed is not None:
            partial_value, summed, returned = lax.optimization_barrier(
                (partial_value, summed, returned)
            )
        else:
            partial_value, lora_left = lax.optimization_barrier((partial_value, lora_left))
        following = lax.psum_scatter(partial_value, "seq", scatter_dimension=0, tiled=False)
        if summed is None:
            lora_left = lax.all_to_all(lora_left, "exp", split_axis=0, concat_axis=0, tiled=True)
            gate_grad, up_grad, lora_left = lax.optimization_barrier(
                (gate_grad, up_grad, lora_left)
            )
        else:
            send_back(summed)
        start, summed = start + piece, following
    send_back(summed)
    moe_parts = [
        matmul(merge, block.reshape(experts * capacity, -1)) for block in returned
    ]
    moe_grad = jnp.concatenate(moe_parts, axis=1)

    scale = lax.dynamic_slice_in_dim(norm_scale_vector, my_seq * quarter, quarter, 0)
    adapter = lax.dynamic_slice_in_dim(adapter_up_matrix, my_seq * quarter, quarter, 1)
    residual_f32 = residual.astype(jnp.float32)
    scaled = scale.astype(jnp.float32)[None, :] * moe_grad
    sums = jnp.concatenate(
        [
            contract_trailing(grad, adapter),
            contract_trailing(residual, adapter),
            contract_trailing(scaled.astype(jnp.bfloat16), adapter),
            jnp.sum(residual_f32 * residual_f32, axis=1, keepdims=True),
            jnp.sum(scaled * residual_f32, axis=1, keepdims=True),
            jnp.zeros((group, LANES - 3 * rank - 2), jnp.float32),
        ],
        axis=1,
    )
    sums = lax.psum(sums, "seq")
    inverse_rms = lax.rsqrt(sums[:, 3 * rank : 3 * rank + 1] / width + NORM_EPS)
    back = sums[:, 3 * rank + 1 : 3 * rank + 2] / width * inverse_rms**3
    hidden_state = (
        grad.astype(jnp.float32) + inverse_rms * scaled - residual_f32 * back
    ).astype(jnp.bfloat16)
    act = ADAPTER_SCALE * (
        sums[:, :rank]
        + inverse_rms * sums[:, 2 * rank : 3 * rank]
        - back * sums[:, rank : 2 * rank]
    )
    act = act.astype(jnp.bfloat16)
    lora_right = jnp.concatenate(
        [
            hidden_state.reshape(group, n_exp, hid_piece),
            jnp.zeros((group, n_exp, att_piece - hid_piece), jnp.bfloat16),
            jnp.broadcast_to(act[:, None], (group, n_exp, rank)),
            jnp.zeros((group, n_exp, LANES - att_piece - rank), jnp.bfloat16),
        ],
        axis=2,
    ).transpose(1, 0, 2)
    lora_right = lax.all_to_all(lora_right, "exp", split_axis=0, concat_axis=0, tiled=True)
    products = contract_leading(
        lora_left.reshape(-1, LANES), lora_right.reshape(-1, LANES)
    )
    down_rows = products[:att_piece, att_piece : att_piece + rank]
    up_rows = ADAPTER_SCALE * products[att_piece : att_piece + rank, :hid_piece].T
    total = jnp.concatenate([down_rows, up_rows], axis=0)
    members = n_exp * n_seq
    route = [
        (member, (member % n_seq) * n_exp + member // n_seq) for member in range(members)
    ]
    total = lax.ppermute(total, ("exp", "seq"), route)
    hidden_rows = lax.all_to_all(
        hidden_state.reshape(n_seq, tokens, quarter),
        "seq",
        split_axis=0,
        concat_axis=0,
        tiled=True,
    )
    hidden_rows = hidden_rows.transpose(1, 0, 2).reshape(tokens, width)
    return (
        hidden_rows,
        total[:att_piece],
        total[att_piece:],
    )


def solution(mesh):
    return jax.shard_map(
        per_device,
        mesh=mesh,
        in_specs=(
            P(("exp", "seq"), None),
            P(("exp", "seq"), None),
            P(),
            P(("exp", "seq"), None),
            P(("exp", "seq"), None),
            P("exp", None, "seq"),
            P("exp", None, "seq"),
            P("exp", "seq", None),
            P("exp", None, "seq"),
            P("exp", None, "seq"),
            P(("exp", "seq"), None),
            P(("exp", "seq"), None),
            P(),
        ),
        out_specs=(P(("exp", "seq"), None), P(("exp", "seq"), None), P(("exp", "seq"), None)),
        check_vma=False,
    )
```

```python
import functools

import jax
import jax.numpy as jnp
from jax import lax
from jax.experimental import pallas as pl
from jax.experimental.pallas import tpu as pltpu
from jax.sharding import PartitionSpec as P

ADAPTER_SCALE = 2.0
NORM_EPS = 1e-06
LANES = 128
BACK_TILES = (9, 5)
MESH = pl.DeviceIdType.MESH


def silu_parts(gate_val):
    sigmoid_val = jax.nn.sigmoid(gate_val)
    return (gate_val * sigmoid_val, sigmoid_val * (1.0 + gate_val * (1.0 - sigmoid_val)))


def contract_trailing(left, right):
    return lax.dot_general(
        left, right, (((1,), (1,)), ((), ())), preferred_element_type=jnp.float32
    )


def contract_leading(left, right):
    return lax.dot_general(
        left, right, (((0,), (0,)), ((), ())), preferred_element_type=jnp.float32
    )


def matmul(left, right):
    return lax.dot_general(
        left, right, (((1,), (0,)), ((), ())), preferred_element_type=jnp.float32
    )


def by_column(array, parts):
    rows, columns = array.shape
    return array.reshape(rows, parts, columns // parts).transpose(1, 0, 2)


def dispatch_kernel(
    n_exp, n_seq, outgoing, rows, own_sem, send_sem, recv_sem, side_send, right_sem, left_sem,
    far_send, far_sem,
):
    me, seq = lax.axis_index("exp"), lax.axis_index("seq")
    right, left = lax.rem(seq + 1, n_seq), lax.rem(seq + n_seq - 1, n_seq)

    barrier = pltpu.get_barrier_semaphore()

    def greet(offset, carry):
        pl.semaphore_signal(
            barrier, inc=1, device_id=(lax.rem(me + offset, n_exp), seq), device_id_type=MESH
        )
        return carry

    lax.fori_loop(1, n_exp, greet, 0)
    for other in (right, left):
        pl.semaphore_signal(barrier, inc=1, device_id=(me, other), device_id_type=MESH)
    pl.semaphore_wait(barrier, n_exp + 1)

    own = pltpu.make_async_copy(outgoing.at[me], rows.at[seq, me], own_sem)
    own.start()

    def over_exp(offset):
        other = lax.rem(me + offset, n_exp)
        return pltpu.make_async_remote_copy(
            src_ref=outgoing.at[other],
            dst_ref=rows.at[seq, me],
            send_sem=send_sem.at[offset],
            recv_sem=recv_sem.at[offset],
            device_id=(other, seq),
            device_id_type=MESH,
        )

    def start_over_exp(offset, carry):
        over_exp(offset).start()
        return carry

    lax.fori_loop(1, n_exp, start_over_exp, 0)
    own.wait()

    def beside(offset, towards, columns, send, recv):
        block = rows.at[columns, lax.rem(me - offset + n_exp, n_exp)]
        return pltpu.make_async_remote_copy(
            src_ref=block,
            dst_ref=block,
            send_sem=send,
            recv_sem=recv,
            device_id=(me, towards),
            device_id_type=MESH,
        )

    def to_right(offset):
        return beside(offset, right, seq, side_send.at[0, offset], right_sem.at[offset])

    def to_left(offset):
        return beside(offset, left, seq, side_send.at[1, offset], left_sem.at[offset])

    def onward_right(offset):
        return beside(offset, right, left, far_send.at[offset], far_sem.at[offset])

    def onward_left(offset):
        return beside(offset, left, right, far_send.at[offset], far_sem.at[offset])

    def spread(offset):
        to_right(offset).start()
        to_left(offset).start()

    def onward(pair):
        to_right(2 * pair).wait_recv()
        onward_right(2 * pair).start()
        to_left(2 * pair).wait_recv()
        to_right(2 * pair + 1).wait_recv()
        to_left(2 * pair + 1).wait_recv()
        onward_left(2 * pair + 1).start()

    def arrive(offset):
        over_exp(offset).wait_recv()
        spread(offset)

    spread(0)
    arrive(1)

    def step(pair, carry):
        arrive(2 * pair)
        arrive(2 * pair + 1)
        onward(pair - 1)
        return carry

    lax.fori_loop(1, n_exp // 2, step, 0)
    onward(n_exp // 2 - 1)

    def finish(pair, carry):
        for offset in (2 * pair, 2 * pair + 1):
            to_right(offset).wait_send()
            to_left(offset).wait_send()
        onward_right(2 * pair).wait()
        onward_left(2 * pair + 1).wait()
        return carry

    lax.fori_loop(0, n_exp // 2, finish, 0)

    def sent(offset, carry):
        over_exp(offset).wait_send()
        return carry

    lax.fori_loop(1, n_exp, sent, 0)


def dispatch(outgoing, n_exp, n_seq):
    return pl.pallas_call(
        functools.partial(dispatch_kernel, n_exp, n_seq),
        out_shape=jax.ShapeDtypeStruct((n_seq,) + outgoing.shape, outgoing.dtype),
        in_specs=[pl.BlockSpec(memory_space=pl.ANY)],
        out_specs=pl.BlockSpec(memory_space=pl.ANY),
        scratch_shapes=[
            pltpu.SemaphoreType.DMA,
            pltpu.SemaphoreType.DMA((n_exp,)),
            pltpu.SemaphoreType.DMA((n_exp,)),
            pltpu.SemaphoreType.DMA((2, n_exp)),
            pltpu.SemaphoreType.DMA((n_exp,)),
            pltpu.SemaphoreType.DMA((n_exp,)),
            pltpu.SemaphoreType.DMA((n_exp,)),
            pltpu.SemaphoreType.DMA((n_exp,)),
        ],
        compiler_params=pltpu.CompilerParams(
            collective_id=0, has_side_effects=True, vmem_limit_bytes=1 << 20
        ),
    )(outgoing)


def exchange_kernel(n_exp, blocks, landed, own_sem, send_sem, recv_sem):
    me, seq = lax.axis_index("exp"), lax.axis_index("seq")
    barrier = pltpu.get_barrier_semaphore()

    def greet(offset, carry):
        pl.semaphore_signal(
            barrier, inc=1, device_id=(lax.rem(me + offset, n_exp), seq), device_id_type=MESH
        )
        return carry

    lax.fori_loop(1, n_exp, greet, 0)
    pl.semaphore_wait(barrier, n_exp - 1)
    own = pltpu.make_async_copy(blocks.at[me], landed.at[me], own_sem)
    own.start()

    def over_exp(offset):
        other = lax.rem(me + offset, n_exp)
        return pltpu.make_async_remote_copy(
            src_ref=blocks.at[other],
            dst_ref=landed.at[me],
            send_sem=send_sem.at[offset],
            recv_sem=recv_sem.at[offset],
            device_id=(other, seq),
            device_id_type=MESH,
        )

    def start(offset, carry):
        over_exp(offset).start()
        return carry

    def finish(offset, carry):
        over_exp(offset).wait()
        return carry

    lax.fori_loop(1, n_exp, start, 0)
    own.wait()
    lax.fori_loop(1, n_exp, finish, 0)


def exchange(blocks, n_exp, collective_id):
    return pl.pallas_call(
        functools.partial(exchange_kernel, n_exp),
        out_shape=jax.ShapeDtypeStruct(blocks.shape, blocks.dtype),
        in_specs=[pl.BlockSpec(memory_space=pl.ANY)],
        out_specs=pl.BlockSpec(memory_space=pl.ANY),
        scratch_shapes=[
            pltpu.SemaphoreType.DMA,
            pltpu.SemaphoreType.DMA((n_exp,)),
            pltpu.SemaphoreType.DMA((n_exp,)),
        ],
        compiler_params=pltpu.CompilerParams(
            collective_id=collective_id, has_side_effects=True, vmem_limit_bytes=1 << 20
        ),
        cost_estimate=pl.CostEstimate(flops=0, bytes_accessed=50_000_000, transcendentals=0),
    )(blocks)


def per_device(
    layer_output_gradient,
    residual_input,
    norm_scale_vector,
    chosen_expert_index,
    routing_gate_weight,
    expert_gate_weight,
    expert_up_weight,
    expert_down_weight,
    stored_gate_state,
    stored_up_state,
    attention_output,
    saved_adapter_latent,
    adapter_up_matrix,
):
    n_exp, n_seq = lax.axis_size("exp"), lax.axis_size("seq")
    my_seq = lax.axis_index("seq")
    tokens, width = layer_output_gradient.shape
    top_count = chosen_expert_index.shape[1]
    rank = saved_adapter_latent.shape[1]
    experts = n_exp * expert_gate_weight.shape[0]
    capacity = stored_gate_state.shape[1] // experts
    heads_width = attention_output.shape[1]
    quarter, att_quarter = width // n_seq, heads_width // n_seq
    group = tokens * n_seq

    small = jnp.concatenate(
        [
            saved_adapter_latent,
            chosen_expert_index.astype(jnp.bfloat16),
            routing_gate_weight,
            jnp.zeros((tokens, LANES - rank - 2 * top_count), jnp.bfloat16),
        ],
        axis=1,
    )
    packed = jnp.concatenate(
        [
            by_column(layer_output_gradient, n_seq),
            by_column(residual_input, n_seq),
            by_column(attention_output, n_seq),
            jnp.broadcast_to(small[None], (n_seq, tokens, LANES)),
        ],
        axis=2,
    )
    packed = lax.all_to_all(packed, "seq", split_axis=0, concat_axis=0, tiled=True)
    packed = packed.reshape(group, -1)
    grad = packed[:, :quarter]
    residual = packed[:, quarter : 2 * quarter]
    attention = packed[:, 2 * quarter : 2 * quarter + att_quarter]
    small = packed[:, 2 * quarter + att_quarter :]
    latent = small[:, :rank]
    ids = small[:, rank : rank + top_count].astype(jnp.int32)
    weights = small[:, rank + top_count : rank + 2 * top_count].astype(jnp.float32)

    labels = jnp.arange(experts, dtype=jnp.int32)
    hits = (ids[:, :, None] == labels[None, None, :]).astype(jnp.float32)
    named = jnp.sum(hits, axis=1)
    named_weight = jnp.sum(hits * weights[:, :, None], axis=1)
    before = jnp.sum(
        jnp.where(
            jnp.arange(group)[:, None, None] > jnp.arange(group)[None, :, None], named[None], 0.0
        ),
        axis=1,
    )
    slot_of = jnp.where(named > 0.0, before.astype(jnp.int32), -1)
    taken = slot_of[:, :, None] == jnp.arange(capacity, dtype=jnp.int32)[None, None, :]
    taken = taken.reshape(group, experts * capacity)
    pick = taken.astype(jnp.bfloat16)
    spread = jnp.repeat(named_weight, capacity, axis=1)
    merge = jnp.where(taken, spread, 0.0).astype(jnp.bfloat16)

    att_piece, hid_piece = att_quarter // n_exp, quarter // n_exp
    lora_left = jnp.concatenate(
        [
            attention.reshape(group, n_exp, att_piece),
            jnp.broadcast_to(latent[:, None], (group, n_exp, rank)),
            jnp.zeros((group, n_exp, LANES - att_piece - rank), jnp.bfloat16),
        ],
        axis=2,
    ).transpose(1, 0, 2)

    down = expert_down_weight[0]
    outgoing = contract_leading(pick, grad).astype(jnp.bfloat16)
    rows = dispatch(outgoing.reshape(experts, capacity, quarter), n_exp, n_seq)
    rows = rows.reshape(n_seq, -1, quarter)
    hidden_grad = None
    for source in range(n_seq):
        term = contract_trailing(rows[source], down[:, source * quarter : (source + 1) * quarter])
        hidden_grad = term if hidden_grad is None else hidden_grad + term
    activation, silu_slope = silu_parts(stored_gate_state[0].astype(jnp.float32))
    gate_grad = (hidden_grad * stored_up_state[0].astype(jnp.float32) * silu_slope).astype(
        jnp.bfloat16
    )
    up_grad = (hidden_grad * activation).astype(jnp.bfloat16)

    returned = []

    def send_back(summed):
        returned.append(
            exchange(summed.reshape(experts, capacity, -1), n_exp, 1 + len(returned))
        )

    start, summed = 0, None
    for tiles in BACK_TILES:
        piece = tiles * LANES
        pieces = []
        for source in range(n_seq):
            first = source * quarter + start
            value = contract_trailing(
                gate_grad, expert_gate_weight[0, first : first + piece]
            ) + contract_trailing(up_grad, expert_up_weight[0, first : first + piece])
            pieces.append(value.astype(jnp.bfloat16))
        partial_value = jnp.stack(pieces)
        if summed is not None:
            partial_value, summed, returned = lax.optimization_barrier(
                (partial_value, summed, returned)
            )
        else:
            partial_value, lora_left = lax.optimization_barrier((partial_value, lora_left))
        following = lax.psum_scatter(partial_value, "seq", scatter_dimension=0, tiled=False)
        if summed is None:
            lora_left = lax.all_to_all(lora_left, "exp", split_axis=0, concat_axis=0, tiled=True)
            gate_grad, up_grad, lora_left = lax.optimization_barrier(
                (gate_grad, up_grad, lora_left)
            )
        else:
            send_back(summed)
        start, summed = start + piece, following
    send_back(summed)
    moe_parts = [
        matmul(merge, block.reshape(experts * capacity, -1)) for block in returned
    ]
    moe_grad = jnp.concatenate(moe_parts, axis=1)

    scale = lax.dynamic_slice_in_dim(norm_scale_vector, my_seq * quarter, quarter, 0)
    adapter = lax.dynamic_slice_in_dim(adapter_up_matrix, my_seq * quarter, quarter, 1)
    residual_f32 = residual.astype(jnp.float32)
    scaled = scale.astype(jnp.float32)[None, :] * moe_grad
    sums = jnp.concatenate(
        [
            contract_trailing(grad, adapter),
            contract_trailing(residual, adapter),
            contract_trailing(scaled.astype(jnp.bfloat16), adapter),
            jnp.sum(residual_f32 * residual_f32, axis=1, keepdims=True),
            jnp.sum(scaled * residual_f32, axis=1, keepdims=True),
            jnp.zeros((group, LANES - 3 * rank - 2), jnp.float32),
        ],
        axis=1,
    )
    sums = lax.psum(sums, "seq")
    inverse_rms = lax.rsqrt(sums[:, 3 * rank : 3 * rank + 1] / width + NORM_EPS)
    back = sums[:, 3 * rank + 1 : 3 * rank + 2] / width * inverse_rms**3
    hidden_state = (
        grad.astype(jnp.float32) + inverse_rms * scaled - residual_f32 * back
    ).astype(jnp.bfloat16)
    act = ADAPTER_SCALE * (
        sums[:, :rank]
        + inverse_rms * sums[:, 2 * rank : 3 * rank]
        - back * sums[:, rank : 2 * rank]
    )
    act = act.astype(jnp.bfloat16)
    lora_right = jnp.concatenate(
        [
            hidden_state.reshape(group, n_exp, hid_piece),
            jnp.zeros((group, n_exp, att_piece - hid_piece), jnp.bfloat16),
            jnp.broadcast_to(act[:, None], (group, n_exp, rank)),
            jnp.zeros((group, n_exp, LANES - att_piece - rank), jnp.bfloat16),
        ],
        axis=2,
    ).transpose(1, 0, 2)
    lora_right = exchange(lora_right, n_exp, 1 + len(BACK_TILES))
    products = contract_leading(
        lora_left.reshape(-1, LANES), lora_right.reshape(-1, LANES)
    )
    down_rows = products[:att_piece, att_piece : att_piece + rank]
    up_rows = ADAPTER_SCALE * products[att_piece : att_piece + rank, :hid_piece].T
    total = jnp.concatenate([down_rows, up_rows], axis=0)
    members = n_exp * n_seq
    route = [
        (member, (member % n_seq) * n_exp + member // n_seq) for member in range(members)
    ]
    total = lax.ppermute(total, ("exp", "seq"), route)
    hidden_rows = lax.all_to_all(
        hidden_state.reshape(n_seq, tokens, quarter),
        "seq",
        split_axis=0,
        concat_axis=0,
        tiled=True,
    )
    hidden_rows = hidden_rows.transpose(1, 0, 2).reshape(tokens, width)
    return (
        hidden_rows,
        total[:att_piece],
        total[att_piece:],
    )


def solution(mesh):
    return jax.shard_map(
        per_device,
        mesh=mesh,
        in_specs=(
            P(("exp", "seq"), None),
            P(("exp", "seq"), None),
            P(),
            P(("exp", "seq"), None),
            P(("exp", "seq"), None),
            P("exp", None, "seq"),
            P("exp", None, "seq"),
            P("exp", "seq", None),
            P("exp", None, "seq"),
            P("exp", None, "seq"),
            P(("exp", "seq"), None),
            P(("exp", "seq"), None),
            P(),
        ),
        out_specs=(P(("exp", "seq"), None), P(("exp", "seq"), None), P(("exp", "seq"), None)),
        check_vma=False,
    )
```
